32 devices in a mesh: ctx: 4 (over z), head: 8 (over y, x, core).
Axes of the slice: x: 2, y: 2, z: 4, core: 2. Of those that a mesh axis runs over, the one named last changes fastest.
Arguments:
- query_rows: bfloat16 [8192, 4096], P('ctx', 'head'), may hold values from -6 to 6
- key_rows: bfloat16 [8192, 4096], P('ctx', 'head'), may hold values from -6 to 6
- value_rows: bfloat16 [8192, 4096], P('ctx', 'head'), may hold values from -6 to 6
- out_grad: bfloat16 [8192, 4096], P('ctx', 'head'), may hold values from -6 to 6
- hub_blocks: int32 [2], replicated, may hold values from 0 to 63, as said below
- local_lists: int32 [64, 6], replicated, may hold values from -3 to 3
Outputs:
- attended: bfloat16 [8192, 4096], P('ctx', 'head')
- query_gradient: bfloat16 [8192, 4096], P('ctx', 'head')
- key_grad: bfloat16 [8192, 4096], P('ctx', 'head')
- value_grad: bfloat16 [8192, 4096], P('ctx', 'head')
The draws below stay inside these ranges and needn't reach their ends.
Inputs may be any that keep to these rules, and one draw needn't show every extreme that they name: `hub_blocks`: 2 distinct block numbers.
All inputs are finite; a program needn't handle non-finite values.
Results may differ from the reference program's by a relative error of at most 0.012.
The reference program's roundings to bfloat16 on the way count: a program that leaves them out, or rounds other values in their place, can miss the bound.
Values may be sent and summed in bfloat16 or wider, within the bound.
A program may use at most 192 MiB of HBM per device.

```python
import math
import jax
import jax.numpy as jnp
from jax import lax

HEADS = 32
DH = 128
BLK = 128
HB = 3
LIST = 6
NBLK = 64
SEQ = 8192


def hub_pick(key):
    other_block = jax.random.randint(jax.random.fold_in(key, 11), (), 0, NBLK - 1).astype(jnp.int32)
    last_block = jnp.full((), NBLK - 1, dtype=jnp.int32)
    swapped = jax.random.randint(jax.random.fold_in(key, 12), (), 0, 2).astype(jnp.int32)
    first_hub = jnp.where(swapped == 1, other_block, last_block)
    second_hub = jnp.where(swapped == 1, last_block, other_block)
    return jnp.stack([first_hub, second_hub]).astype(jnp.int32)


def draw_hub_blocks(key, part):
    return hub_pick(key)


def draw_query_rows(key, part):
    background = jax.random.normal(jax.random.fold_in(key, 21), (SEQ, HEADS * DH), jnp.float32)
    return jnp.clip(background, -6.0, 6.0).astype(jnp.bfloat16)


def draw_key_rows(key, part):
    background = jax.random.normal(jax.random.fold_in(key, 22), (SEQ, HEADS * DH), jnp.float32)
    return jnp.clip(background, -6.0, 6.0).astype(jnp.bfloat16)


def place_ends(entries, rng, low, top_value):
    longest = entries.shape.index(max(entries.shape))
    spots = []
    for shift in (0, 1):
        where = [jax.random.randint(jax.random.fold_in(rng, axis), (), 0, length) for axis, length in enumerate(entries.shape)]
        where[longest] = (where[longest] + shift) % entries.shape[longest]
        spots.append(tuple(where))
    return entries.at[spots[0]].set(low).at[spots[1]].set(top_value)


def levels(key, dims, split, low, largest):
    def one(dim, parts):
        heights = jax.random.uniform(jax.random.fold_in(jax.random.fold_in(key, 6), dim), (parts,), jnp.float32, low / len(split), largest / len(split))
        return jnp.repeat(jnp.exp(heights), dims[dim] // parts).reshape((-1,) + (1,) * (len(dims) - dim - 1))

    loudness = one(*split[0])
    for cut in split[1:]:
        loudness = loudness * one(*cut)
    return loudness


def gaussian(rng, dims, scale, bound, cuts=(), kind=jnp.bfloat16):
    entries = scale * jax.random.normal(rng, dims, jnp.float32)
    if cuts:
        entries = entries * levels(rng, dims, cuts, -0.22, 0.18)
    return jnp.clip(entries, -bound, bound).astype(kind)


def setup_inputs(seed: int = 0) -> dict:
    keys = jax.random.split(jax.random.key(seed), 7)
    query_rows = draw_query_rows(jax.random.fold_in(keys[6], 71), 0)
    key_rows = draw_key_rows(jax.random.fold_in(keys[6], 71), 0)
    value_rows = gaussian(keys[2], (SEQ, HEADS * DH), 1.0, 6.0, ((0, 4), (1, 8)))
    out_grad = gaussian(keys[3], (SEQ, HEADS * DH), 1.0, 6.0, ((0, 4), (1, 8)))
    hub_blocks = draw_hub_blocks(jax.random.fold_in(keys[6], 71), 0)
    local_lists = place_ends(jax.random.randint(keys[5], (NBLK, LIST), 0 - HB, HB + 1), jax.random.fold_in(keys[5], 1), 0 - HB, HB).astype(jnp.int32)
    return dict(query_rows=query_rows, key_rows=key_rows, value_rows=value_rows, out_grad=out_grad, hub_blocks=hub_blocks, local_lists=local_lists)


def key_table(local_lists, hub_blocks):
    block_count = local_lists.shape[0]
    listed = jnp.arange(block_count, dtype=jnp.int32)[:, None] + local_lists.astype(jnp.int32)
    inside = (listed >= 0) & (listed < block_count)
    hub_cols = jnp.broadcast_to(hub_blocks.astype(jnp.int32)[None, :], (block_count, hub_blocks.shape[0]))
    table = jnp.concatenate([jnp.clip(listed, 0, block_count - 1), hub_cols], axis=1).astype(jnp.int32)
    living = jnp.concatenate([inside, jnp.ones(hub_cols.shape, dtype=bool)], axis=1)
    return (table, living)

def reference(query_rows, key_rows, value_rows, out_grad, hub_blocks, local_lists):
    score_scale = 1.0 / math.sqrt(DH)
    table, living = key_table(local_lists, hub_blocks)
    flat_table = table.reshape(-1)
    weight_keep_mask = living.astype(jnp.float32)[:, :, None, None]

    def split_heads(source):
        return jnp.transpose(source.reshape(NBLK, BLK, HEADS, DH), (2, 0, 1, 3))

    def join_heads(source):
        return jnp.transpose(source, (1, 2, 0, 3)).reshape(SEQ, HEADS * DH)

    def one_head(members):
        query_head, key_head, value_head, grad_head = members
        query_wide = query_head.astype(jnp.float32)
        gradient_wide = grad_head.astype(jnp.float32)
        key_block_set = key_head[table].astype(jnp.float32)
        value_block_set = value_head[table].astype(jnp.float32)
        logit_scores = jnp.einsum('ahw,amtw->ahmt', query_wide, key_block_set) * score_scale
        logit_scores = jnp.where(living[:, None, :, None], logit_scores, -1e+30)
        highest = lax.optimization_barrier(jnp.max(logit_scores, axis=(2, 3), keepdims=True))
        log_norm = highest + jnp.log(lax.optimization_barrier(jnp.sum(jnp.exp(logit_scores - highest), axis=(2, 3), keepdims=True)))
        chances = jnp.exp(logit_scores - log_norm)
        rounded_values = lax.optimization_barrier(chances.astype(jnp.bfloat16)).astype(jnp.float32)
        attended = jnp.einsum('nytu,ntua->nya', rounded_values, value_block_set).astype(jnp.bfloat16)
        offsets = lax.optimization_barrier(jnp.sum(gradient_wide * attended.astype(jnp.float32), axis=2))
        shifted_entries = jnp.einsum('ahw,amtw->ahmt', gradient_wide, value_block_set)
        decay_slopes = chances * (shifted_entries - offsets[:, :, None, None]) * score_scale
        decay_slopes = lax.optimization_barrier(decay_slopes.astype(jnp.bfloat16)).astype(jnp.float32)
        query_gradient = jnp.einsum('nytu,ntua->nya', decay_slopes, key_block_set).astype(jnp.bfloat16)
        key_pieces = jnp.einsum('fvil,fvw->filw', decay_slopes, query_wide) * weight_keep_mask
        value_pieces = jnp.einsum('fvil,fvw->filw', rounded_values, gradient_wide) * weight_keep_mask
        key_grad = jax.ops.segment_sum(key_pieces.reshape(-1, BLK, DH), flat_table, num_segments=NBLK)
        value_grad = jax.ops.segment_sum(value_pieces.reshape(-1, BLK, DH), flat_table, num_segments=NBLK)
        return (attended, query_gradient, key_grad.astype(jnp.bfloat16), value_grad.astype(jnp.bfloat16))
    attended, query_gradient, key_grad, value_grad = lax.map(one_head, (split_heads(query_rows), split_heads(key_rows), split_heads(value_rows), split_heads(out_grad)))
    return (join_heads(attended), join_heads(query_gradient), join_heads(key_grad), join_heads(value_grad))
```

```python
import functools
import math

import jax
import jax.numpy as jnp
from jax import lax
from jax.experimental import pallas as pl
from jax.experimental.pallas import tpu as pltpu
from jax.sharding import PartitionSpec as P

DH = 128
BLK = 128
HB = 3
G = 2
DEAD = -1e30


def attend_kernel(
    total_blocks,
    listed,
    width,
    lists_ref,
    q_ref,
    k_ref,
    v_ref,
    g_ref,
    left_ref,
    right_ref,
    hub_ref,
    att_ref,
    dq_ref,
    dk_ref,
    dv_ref,
    dleft_ref,
    dright_ref,
    dhub_ref,
    kx,
    vx,
    kt,
    vt,
    dka,
    dva,
):
    blocks = q_ref.shape[0]
    extended = blocks + 2 * HB
    store = extended + G
    heads = width // DH
    scale = 1.0 / math.sqrt(DH)
    c = scale * math.log2(math.e)
    first_block = lax.axis_index("ctx") * blocks

    kx[0:HB] = left_ref[0]
    vx[0:HB] = left_ref[1]
    kx[HB : HB + blocks] = k_ref[...]
    vx[HB : HB + blocks] = v_ref[...]
    kx[HB + blocks : extended] = right_ref[0]
    vx[HB + blocks : extended] = right_ref[1]
    kx[extended:store] = hub_ref[0]
    vx[extended:store] = hub_ref[1]

    def flip(i, carry):
        for h in range(heads):
            hs = slice(h * DH, (h + 1) * DH)
            kt[i, h] = kx[i, :, hs].T
            vt[i, h] = vx[i, :, hs].T
            dka[i, h] = jnp.zeros((BLK, DH), jnp.float32)
            dva[i, h] = jnp.zeros((BLK, DH), jnp.float32)
        return carry

    lax.fori_loop(0, store, flip, 0)

    def body(b, carry):
        spots = []
        bias = []
        for j in range(listed):
            offset = lists_ref[first_block + b, j]
            there = first_block + b + offset
            alive = (there >= 0) & (there < total_blocks)
            spots.append(HB + b + offset)
            bias.append(jnp.where(alive, 0.0, DEAD))
        for j in range(G):
            spots.append(extended + j)
            bias.append(0.0)
        n = len(spots)
        for h in range(heads):
            hs = slice(h * DH, (h + 1) * DH)
            q = q_ref[b, :, hs]
            g = g_ref[b, :, hs]
            qt = q.T
            gt = g.T
            keys = jnp.concatenate([kx[i, :, hs] for i in spots], axis=0)
            s = jnp.dot(keys, qt, preferred_element_type=jnp.float32)
            parts = [s[e * BLK : (e + 1) * BLK] for e in range(n)]
            tops = [jnp.max(parts[e], axis=0, keepdims=True) * c + bias[e] for e in range(n)]
            top = functools.reduce(jnp.maximum, tops)
            ps = [jnp.exp2(parts[e] * c + (bias[e] - top)) for e in range(n)]
            total = functools.reduce(
                jnp.add, [jnp.sum(p, axis=0, keepdims=True) for p in ps]
            )
            inverse = 1.0 / total
            chances = jnp.concatenate(ps, axis=0) * inverse
            weights = chances.astype(jnp.bfloat16)
            values_t = jnp.concatenate([vt[i, h] for i in spots], axis=1)
            mixed_t = jnp.dot(values_t, weights, preferred_element_type=jnp.float32)
            mixed = mixed_t.T.astype(jnp.bfloat16)
            att_ref[b, :, hs] = mixed
            rounded = mixed_t.astype(jnp.bfloat16).astype(jnp.float32)
            offsets = jnp.sum(gt.astype(jnp.float32) * rounded, axis=0, keepdims=True)
            values = jnp.concatenate([vx[i, :, hs] for i in spots], axis=0)
            pushed = jnp.dot(values, gt, preferred_element_type=jnp.float32)
            slopes = (chances * (pushed - offsets)).astype(jnp.bfloat16)
            keys_t = jnp.concatenate([kt[i, h] for i in spots], axis=1)
            dq_t = jnp.dot(keys_t, slopes, preferred_element_type=jnp.float32) * scale
            dq_ref[b, :, hs] = dq_t.T.astype(jnp.bfloat16)
            dk_part = jnp.dot(slopes, q, preferred_element_type=jnp.float32)
            dv_part = jnp.dot(weights, g, preferred_element_type=jnp.float32)
            for e in range(n):
                dka[spots[e], h] += dk_part[e * BLK : (e + 1) * BLK]
                dva[spots[e], h] += dv_part[e * BLK : (e + 1) * BLK]
        return carry

    lax.fori_loop(0, blocks, body, 0)

    for h in range(heads):
        hs = slice(h * DH, (h + 1) * DH)
        dleft_ref[0, :, :, hs] = (dka[0:HB, h] * scale).astype(jnp.bfloat16)
        dleft_ref[1, :, :, hs] = dva[0:HB, h].astype(jnp.bfloat16)
        dright_ref[0, :, :, hs] = (dka[HB + blocks : extended, h] * scale).astype(jnp.bfloat16)
        dright_ref[1, :, :, hs] = dva[HB + blocks : extended, h].astype(jnp.bfloat16)
        dhub_ref[0, :, :, hs] = (dka[extended:store, h] * scale).astype(dhub_ref.dtype)
        dhub_ref[1, :, :, hs] = dva[extended:store, h].astype(dhub_ref.dtype)

    def finish(i, carry):
        for h in range(heads):
            hs = slice(h * DH, (h + 1) * DH)
            dk_ref[i, :, hs] = (dka[HB + i, h] * scale).astype(jnp.bfloat16)
            dv_ref[i, :, hs] = dva[HB + i, h].astype(jnp.bfloat16)
        return carry

    lax.fori_loop(0, blocks, finish, 0)


def attend(local_lists, q, k, v, g, left, right, hub, total_blocks):
    blocks, _, columns = q.shape
    width = 2 * DH if columns % (2 * DH) == 0 else DH
    heads = width // DH
    store = blocks + 2 * HB + G
    whole = pl.BlockSpec((blocks, BLK, width), lambda i: (0, 0, i))
    rim = pl.BlockSpec((2, HB, BLK, width), lambda i: (0, 0, 0, i))
    hubs = pl.BlockSpec((2, G, BLK, width), lambda i: (0, 0, 0, i))
    big = jax.ShapeDtypeStruct(q.shape, jnp.bfloat16)
    rim_shape = jax.ShapeDtypeStruct(left.shape, jnp.bfloat16)
    hub_shape = jax.ShapeDtypeStruct(hub.shape, jnp.float32)
    return pl.pallas_call(
        functools.partial(attend_kernel, total_blocks, local_lists.shape[1], width),
        grid=(columns // width,),
        in_specs=[pl.BlockSpec(memory_space=pltpu.SMEM)] + [whole] * 4 + [rim, rim, hubs],
        out_specs=[whole] * 4 + [rim, rim, hubs],
        out_shape=[big] * 4 + [rim_shape, rim_shape, hub_shape],
        scratch_shapes=[
            pltpu.VMEM((store, BLK, width), jnp.bfloat16),
            pltpu.VMEM((store, BLK, width), jnp.bfloat16),
            pltpu.VMEM((store, heads, DH, BLK), jnp.bfloat16),
            pltpu.VMEM((store, heads, DH, BLK), jnp.bfloat16),
            pltpu.VMEM((store, heads, BLK, DH), jnp.float32),
            pltpu.VMEM((store, heads, BLK, DH), jnp.float32),
        ],
        compiler_params=pltpu.CompilerParams(vmem_limit_bytes=60 << 20),
        name="attend",
    )(local_lists, q, k, v, g, left, right, hub)


def local(query_rows, key_rows, value_rows, out_grad, hub_blocks, local_lists):
    count = lax.axis_size("ctx")
    tok_rows, columns = query_rows.shape
    blocks = tok_rows // BLK
    total_blocks = blocks * count
    first_block = lax.axis_index("ctx") * blocks
    up = [(i, i + 1) for i in range(count - 1)]
    down = [(i + 1, i) for i in range(count - 1)]
    q, k, v, g = (
        a.reshape(blocks, BLK, columns) for a in (query_rows, key_rows, value_rows, out_grad)
    )
    spots = hub_blocks - first_block
    here = (spots >= 0) & (spots < blocks)
    clipped = jnp.clip(spots, 0, blocks - 1)

    def pick(a):
        rows = [
            jnp.where(here[j], lax.dynamic_index_in_dim(a, clipped[j], 0, keepdims=False), 0)
            for j in range(G)
        ]
        return jnp.stack(rows)

    hub = lax.psum(jnp.stack([pick(k), pick(v)]), "ctx")
    left = lax.ppermute(jnp.stack([k[-HB:], v[-HB:]]), "ctx", up)
    right = lax.ppermute(jnp.stack([k[:HB], v[:HB]]), "ctx", down)
    attended, dq, dk, dv, dleft, dright, dhub = attend(
        local_lists, q, k, v, g, left, right, hub, total_blocks
    )
    from_right = lax.ppermute(dleft, "ctx", down)
    from_left = lax.ppermute(dright, "ctx", up)
    hub_total = lax.psum(dhub, "ctx")
    number = jnp.arange(blocks, dtype=jnp.int32)[:, None, None]

    def finish(own, part):
        middle = jnp.zeros((blocks - 2 * HB, BLK, columns), jnp.bfloat16)
        sent = jnp.concatenate([from_left[part], middle, from_right[part]], axis=0)
        out = own.astype(jnp.float32) + sent.astype(jnp.float32)
        for j in range(G):
            out = out + jnp.where(number == spots[j], hub_total[part, j][None], 0.0)
        return out.astype(jnp.bfloat16).reshape(tok_rows, columns)

    return (
        attended.reshape(tok_rows, columns),
        dq.reshape(tok_rows, columns),
        finish(dk, 0),
        finish(dv, 1),
    )


def solution(mesh):
    spec = P("ctx", "head")
    return jax.shard_map(
        local,
        mesh=mesh,
        in_specs=(spec, spec, spec, spec, P(), P()),
        out_specs=(spec, spec, spec, spec),
        check_vma=False,
    )
```

```python
import functools
import math

import jax
import jax.numpy as jnp
from jax import lax
from jax.experimental import pallas as pl
from jax.experimental.pallas import tpu as pltpu
from jax.sharding import PartitionSpec as P

DH = 128
BLK = 128
HB = 3
G = 2
DEAD = -1e30


def attend_kernel(
    listed,
    width,
    chained,
    number_ref,
    spots_ref,
    bias_ref,
    q_ref,
    k_ref,
    v_ref,
    g_ref,
    left_ref,
    right_ref,
    hub_ref,
    *refs,
):
    refs = refs[4:] if chained else refs
    att_ref, dq_ref, dk_ref, dv_ref, dleft_ref, dright_ref, dhub_ref = refs[:7]
    kx, vx, kt, vt, dka, dva = refs[7:]
    blocks = q_ref.shape[0]
    extended = blocks + 2 * HB
    store = extended + G
    heads = width // DH
    scale = 1.0 / math.sqrt(DH)
    c = scale * math.log2(math.e)

    kx[0:HB] = left_ref[0]
    vx[0:HB] = left_ref[1]
    kx[HB : HB + blocks] = k_ref[...]
    vx[HB : HB + blocks] = v_ref[...]
    kx[HB + blocks : extended] = right_ref[0]
    vx[HB + blocks : extended] = right_ref[1]
    kx[extended:store] = hub_ref[0]
    vx[extended:store] = hub_ref[1]

    def flip(i, carry):
        for h in range(heads):
            hs = slice(h * DH, (h + 1) * DH)
            kt[i, h] = kx[i, :, hs].T
            vt[i, h] = vx[i, :, hs].T
            dka[i, h] = jnp.zeros((BLK, DH), jnp.float32)
            dva[i, h] = jnp.zeros((BLK, DH), jnp.float32)
        return carry

    lax.fori_loop(0, store, flip, 0)

    def block(b, kept):
        spots = [HB + b + spots_ref[b, j] for j in range(kept)] + [extended + j for j in range(G)]
        bias = [bias_ref[b, j] for j in range(kept)] + [0.0] * G
        n = len(spots)
        for h in range(heads):
            hs = slice(h * DH, (h + 1) * DH)
            q = q_ref[b, :, hs]
            g = g_ref[b, :, hs]
            qt = q.T
            gt = g.T
            keys = jnp.concatenate([kx[i, :, hs] for i in spots], axis=0)
            s = jnp.dot(keys, qt, preferred_element_type=jnp.float32)
            parts = [s[e * BLK : (e + 1) * BLK] for e in range(n)]
            tops = [jnp.max(parts[e], axis=0, keepdims=True) * c + bias[e] for e in range(n)]
            top = functools.reduce(jnp.maximum, tops)
            ps = [jnp.exp2(parts[e] * c + (bias[e] - top)) for e in range(n)]
            total = functools.reduce(
                jnp.add, [jnp.sum(p, axis=0, keepdims=True) for p in ps]
            )
            inverse = 1.0 / total
            chances = jnp.concatenate(ps, axis=0) * inverse
            weights = chances.astype(jnp.bfloat16)
            values_t = jnp.concatenate([vt[i, h] for i in spots], axis=1)
            mixed_t = jnp.dot(values_t, weights, preferred_element_type=jnp.float32)
            mixed = mixed_t.T.astype(jnp.bfloat16)
            att_ref[b, :, hs] = mixed
            rounded = mixed_t.astype(jnp.bfloat16).astype(jnp.float32)
            offsets = jnp.sum(gt.astype(jnp.float32) * rounded, axis=0, keepdims=True)
            values = jnp.concatenate([vx[i, :, hs] for i in spots], axis=0)
            pushed = jnp.dot(values, gt, preferred_element_type=jnp.float32)
            slopes = (chances * (pushed - offsets)).astype(jnp.bfloat16)
            keys_t = jnp.concatenate([kt[i, h] for i in spots], axis=1)
            dq_t = jnp.dot(keys_t, slopes, preferred_element_type=jnp.float32) * scale
            dq_ref[b, :, hs] = dq_t.T.astype(jnp.bfloat16)
            dk_part = jnp.dot(slopes, q, preferred_element_type=jnp.float32)
            dv_part = jnp.dot(weights, g, preferred_element_type=jnp.float32)
            for e in range(n):
                dka[spots[e], h] += dk_part[e * BLK : (e + 1) * BLK]
                dva[spots[e], h] += dv_part[e * BLK : (e + 1) * BLK]

    sizes = [min(4, listed)] + list(range(5, listed + 1))

    def body(b, carry):
        kept = number_ref[b]
        for at, size in enumerate(sizes):
            fits = kept <= size if at == 0 else kept == size
            pl.when(fits)(functools.partial(block, b, size))
        return carry

    lax.fori_loop(0, blocks, body, 0)

    for h in range(heads):
        hs = slice(h * DH, (h + 1) * DH)
        dleft_ref[0, :, :, hs] = (dka[0:HB, h] * scale).astype(jnp.bfloat16)
        dleft_ref[1, :, :, hs] = dva[0:HB, h].astype(jnp.bfloat16)
        dright_ref[0, :, :, hs] = (dka[HB + blocks : extended, h] * scale).astype(jnp.bfloat16)
        dright_ref[1, :, :, hs] = dva[HB + blocks : extended, h].astype(jnp.bfloat16)
        dhub_ref[0, :, :, hs] = (dka[extended:store, h] * scale).astype(dhub_ref.dtype)
        dhub_ref[1, :, :, hs] = dva[extended:store, h].astype(dhub_ref.dtype)

    def finish(i, carry):
        for h in range(heads):
            hs = slice(h * DH, (h + 1) * DH)
            dk_ref[i, :, hs] = (dka[HB + i, h] * scale).astype(jnp.bfloat16)
            dv_ref[i, :, hs] = dva[HB + i, h].astype(jnp.bfloat16)
        return carry

    lax.fori_loop(0, blocks, finish, 0)


def chain_kernel(x_ref, out_ref, from_left, from_right, to_right, to_left, sends, recvs):
    me = lax.axis_index("ctx")
    count = lax.axis_size("ctx")
    last = count - 1
    chunks = x_ref.shape[0]
    mesh_ids = pl.DeviceIdType.MESH

    barrier = pltpu.get_barrier_semaphore()

    @pl.when(me > 0)
    def _():
        pl.semaphore_signal(barrier, inc=1, device_id={"ctx": me - 1}, device_id_type=mesh_ids)

    @pl.when(me < last)
    def _():
        pl.semaphore_signal(barrier, inc=1, device_id={"ctx": me + 1}, device_id_type=mesh_ids)

    @pl.when((me > 0) & (me < last))
    def _():
        pl.semaphore_wait(barrier, 2)

    @pl.when((me == 0) | (me == last))
    def _():
        pl.semaphore_wait(barrier, 1)

    def rightward(source, i):
        return pltpu.make_async_remote_copy(
            src_ref=source.at[i],
            dst_ref=from_left.at[i],
            send_sem=sends.at[0, i],
            recv_sem=recvs.at[0, i],
            device_id={"ctx": me + 1},
            device_id_type=mesh_ids,
        )

    def leftward(source, i):
        return pltpu.make_async_remote_copy(
            src_ref=source.at[i],
            dst_ref=from_right.at[i],
            send_sem=sends.at[1, i],
            recv_sem=recvs.at[1, i],
            device_id={"ctx": me - 1},
            device_id_type=mesh_ids,
        )

    def step(s, carry):
        i = s - me

        @pl.when((i >= 0) & (i < chunks))
        def _():
            @pl.when(me == 0)
            def _():
                rightward(x_ref, i).start()

            @pl.when(me > 0)
            def _():
                rightward(to_right, i).wait_recv()

            @pl.when((me > 0) & (me < last))
            def _():
                to_right[i] = x_ref[i] + from_left[i]
                rightward(to_right, i).start()

        j = s - (last - me)

        @pl.when((j >= 0) & (j < chunks))
        def _():
            @pl.when(me == last)
            def _():
                leftward(x_ref, j).start()

            @pl.when(me < last)
            def _():
                leftward(to_left, j).wait_recv()

            @pl.when((me > 0) & (me < last))
            def _():
                to_left[j] = x_ref[j] + from_right[j]
                leftward(to_left, j).start()

        return carry

    lax.fori_loop(0, chunks + last, step, 0)

    def close(i, carry):
        own = x_ref[i].astype(jnp.float32)

        @pl.when(me == 0)
        def _():
            out_ref[i] = (own + from_right[i].astype(jnp.float32)).astype(out_ref.dtype)

        @pl.when(me == last)
        def _():
            out_ref[i] = (own + from_left[i].astype(jnp.float32)).astype(out_ref.dtype)

        @pl.when((me > 0) & (me < last))
        def _():
            both = from_left[i].astype(jnp.float32) + from_right[i].astype(jnp.float32)
            out_ref[i] = (own + both).astype(out_ref.dtype)

        @pl.when(me < last)
        def _():
            rightward(to_right, i).wait_send()

        @pl.when(me > 0)
        def _():
            leftward(to_left, i).wait_send()

        return carry

    lax.fori_loop(0, chunks, close, 0)


def chain_sum(a, ident):
    columns = a.shape[-1]
    pieces = 8
    rows = a.size // columns // pieces
    flat = a.reshape(pieces, rows, columns)
    buffer = pltpu.VMEM(flat.shape, flat.dtype)
    out = pl.pallas_call(
        chain_kernel,
        out_shape=jax.ShapeDtypeStruct(flat.shape, flat.dtype),
        in_specs=[pl.BlockSpec(memory_space=pltpu.VMEM)],
        out_specs=pl.BlockSpec(memory_space=pltpu.VMEM),
        scratch_shapes=[buffer] * 4
        + [pltpu.SemaphoreType.DMA((2, pieces)), pltpu.SemaphoreType.DMA((2, pieces))],
        compiler_params=pltpu.CompilerParams(
            collective_id=ident, has_side_effects=True, vmem_limit_bytes=16 << 20
        ),
        cost_estimate=pl.CostEstimate(
            flops=4 * a.size, bytes_accessed=120 * a.size, transcendentals=0
        ),
        name=f"chain{ident}",
    )(flat)
    return out.reshape(a.shape)


def attend(base, width, table, q, k, v, g, left, right, hub, earlier):
    blocks, _, columns = q.shape
    heads = width // DH
    number, offsets, bias = table
    listed = offsets.shape[1]
    store = blocks + 2 * HB + G
    whole = pl.BlockSpec((blocks, BLK, width), lambda i: (0, 0, base))
    rim = pl.BlockSpec((2, HB, BLK, width), lambda i: (0, 0, 0, 0))
    hubs_in = pl.BlockSpec((2, G, BLK, width), lambda i: (0, 0, 0, base))
    hubs = pl.BlockSpec((2, G, BLK, width), lambda i: (0, 0, 0, 0))
    big = jax.ShapeDtypeStruct(q.shape, jnp.bfloat16)
    rim_shape = jax.ShapeDtypeStruct(left.shape, jnp.bfloat16)
    hub_shape = jax.ShapeDtypeStruct((2, G, BLK, width), jnp.bfloat16)
    smem = pl.BlockSpec(memory_space=pltpu.SMEM)
    units = 6 * heads * blocks * (listed + G)
    return pl.pallas_call(
        functools.partial(attend_kernel, listed, width, bool(earlier)),
        grid=(1,),
        in_specs=[smem] * 3
        + [whole] * 4
        + [rim, rim, hubs_in]
        + [pl.BlockSpec(memory_space=pl.ANY)] * len(earlier),
        out_specs=[whole] * 4 + [rim, rim, hubs],
        out_shape=[big] * 4 + [rim_shape, rim_shape, hub_shape],
        input_output_aliases={10 + i: i for i in range(len(earlier))},
        scratch_shapes=[
            pltpu.VMEM((store, BLK, width), jnp.bfloat16),
            pltpu.VMEM((store, BLK, width), jnp.bfloat16),
            pltpu.VMEM((store, heads, DH, BLK), jnp.bfloat16),
            pltpu.VMEM((store, heads, DH, BLK), jnp.bfloat16),
            pltpu.VMEM((store, heads, BLK, DH), jnp.float32),
            pltpu.VMEM((store, heads, BLK, DH), jnp.float32),
        ],
        compiler_params=pltpu.CompilerParams(vmem_limit_bytes=56 << 20),
        cost_estimate=pl.CostEstimate(
            flops=8 * units * 2 * BLK * BLK * DH,
            bytes_accessed=16 * blocks * BLK * width,
            transcendentals=heads * blocks * (listed + G) * BLK * BLK,
        ),
        name="attend",
    )(number, offsets, bias, q, k, v, g, left, right, hub, *earlier)


def entry_table(local_lists, first_block, blocks, total_blocks):
    lists = lax.dynamic_slice_in_dim(local_lists, first_block, blocks, 0)
    listed = lists.shape[1]
    reach = jnp.arange(-HB, HB + 1, dtype=jnp.int32)
    there = first_block + jnp.arange(blocks, dtype=jnp.int32)[:, None] + reach[None, :]
    alive = (there >= 0) & (there < total_blocks)
    times = jnp.sum(lists[:, :, None] == reach[None, None, :], axis=1).astype(jnp.int32)
    times = jnp.where(alive, times, 0)
    kept = times > 0
    before = (reach[None, :] < reach[:, None]).astype(jnp.int32)
    rank = jnp.sum(kept.astype(jnp.int32)[:, None, :] * before[None], axis=2)
    seat = kept[:, None, :] & (rank[:, None, :] == jnp.arange(listed)[None, :, None])
    offsets = jnp.sum(jnp.where(seat, reach[None, None, :], 0), axis=2).astype(jnp.int32)
    seat_times = jnp.sum(jnp.where(seat, times[:, None, :], 0), axis=2)
    bias = jnp.where(
        seat_times > 0, jnp.log2(jnp.maximum(seat_times, 1).astype(jnp.float32)), DEAD
    ).astype(jnp.float32)
    return jnp.sum(kept.astype(jnp.int32), axis=1), offsets, bias


def local(query_rows, key_rows, value_rows, out_grad, hub_blocks, local_lists):
    count = lax.axis_size("ctx")
    tok_rows, columns = query_rows.shape
    blocks = tok_rows // BLK
    total_blocks = blocks * count
    first_block = lax.axis_index("ctx") * blocks
    up = [(i, i + 1) for i in range(count - 1)]
    down = [(i + 1, i) for i in range(count - 1)]
    q, k, v, g = (
        a.reshape(blocks, BLK, columns) for a in (query_rows, key_rows, value_rows, out_grad)
    )
    spots = hub_blocks - first_block
    here = (spots >= 0) & (spots < blocks)
    clipped = jnp.clip(spots, 0, blocks - 1)

    table = entry_table(local_lists, first_block, blocks, total_blocks)
    width = 2 * DH if columns % (2 * DH) == 0 else DH

    def pick(a):
        rows = [
            jnp.where(here[j], lax.dynamic_slice_in_dim(a, clipped[j], 1, 0), 0)
            for j in range(G)
        ]
        return jnp.concatenate(rows, axis=0)

    def rims(base):
        own = slice(base * width, (base + 1) * width)
        low = jnp.stack([k[:HB, :, own], v[:HB, :, own]])
        high = jnp.stack([k[blocks - HB :, :, own], v[blocks - HB :, :, own]])
        return low, high

    def shifted(low, high):
        return lax.ppermute(high, "ctx", up), lax.ppermute(low, "ctx", down)

    earlier = ()
    returned = []
    hub_grads = []
    groups = columns // width
    arrived = shifted(*rims(0))
    hub = chain_sum(jnp.stack([pick(k), pick(v)]), 1)
    for base in range(groups):
        coming = None
        if base + 1 < groups:
            ahead, arrived, hub = lax.optimization_barrier((rims(base + 1), arrived, hub))
            coming = shifted(*ahead)
        done = attend(base, width, table, q, k, v, g, *arrived, hub, earlier)
        arrived = coming
        earlier = done[:4]
        dleft, dright, dhub = done[4:]
        returned.append((lax.ppermute(dright, "ctx", up), lax.ppermute(dleft, "ctx", down)))
        hub_grads.append(dhub)
    dhub = jnp.concatenate(hub_grads, axis=3) if groups > 1 else hub_grads[0]
    hub_total = chain_sum(dhub, 2)
    attended, dq, dk, dv = earlier
    from_left, from_right = (
        jnp.concatenate(pieces, axis=3) if len(pieces) > 1 else pieces[0]
        for pieces in zip(*returned)
    )
    number = jnp.arange(blocks, dtype=jnp.int32)[:, None, None]

    def finish(own, part):
        middle = jnp.zeros((blocks - 2 * HB, BLK, columns), jnp.bfloat16)
        sent = jnp.concatenate([from_left[part], middle, from_right[part]], axis=0)
        out = own.astype(jnp.float32) + sent.astype(jnp.float32)
        for j in range(G):
            chosen = hub_total[part, j][None].astype(jnp.float32)
            out = out + jnp.where(number == spots[j], chosen, 0.0)
        return out.astype(jnp.bfloat16).reshape(tok_rows, columns)

    return (
        attended.reshape(tok_rows, columns),
        dq.reshape(tok_rows, columns),
        finish(dk, 0),
        finish(dv, 1),
    )


def solution(mesh):
    spec = P("ctx", "head")
    return jax.shard_map(
        local,
        mesh=mesh,
        in_specs=(spec, spec, spec, spec, P(), P()),
        out_specs=(spec, spec, spec, spec),
        check_vma=False,
    )
```
